32 devices in a mesh: rows: 8 (over z, y), chan: 4 (over x, core).
Axes of the slice: x: 2, y: 2, z: 4, core: 2. Of those that a mesh axis runs over, the one named last changes fastest.
Arguments:
- radiances: float32 [16, 16384], P('chan', 'rows'), may hold values from -6 to 6
- band: int32 [16384, 1], P('rows'), may hold values from 0 to 7; in each aligned block of 2048 rows (0 to 2047, 2048 to 4095, ...) at most 512 rows name the same one
- row_in_band: int32 [16384], P('rows'), may hold values from 0 to 3
- column: int32 [16384], P('rows'), may hold values from 0 to 1439
Outputs:
- cell_count: int32 [32, 1440], P('rows')
- cell_mean: float32 [16, 32, 1440], P('chan', 'rows')
- cell_var: float32 [16, 32, 1440], P('chan', 'rows')
- cell_spread: float32 [32, 1440], P('rows')
- departure: float32 [16, 16384], P('chan', 'rows')
The draws below stay inside these ranges and needn't reach their ends.
Inputs may be any that keep to these rules, and one draw needn't show every extreme that they name: Within each aligned block of 2048 observations (one scan-time shard) no band is named by more than 512 observations, and in some blocks one band is named by exactly 512.
All inputs are finite; a program needn't handle non-finite values.
Results may differ from the reference program's by a relative error of at most 0.0003.
Values sent between devices are 32-bit elements.
A program may use at most 64 MiB of HBM per device.

```python
import math
import jax
import jax.numpy as jnp
import numpy as np
from jax import lax

CHAN = 16
COLS = 1440
ROWS_DEV = 4
OBS_DEV = 2048
LATS = 32
OBS = 16384
CAP = 512
N_ROWS = 8


def touch_ends(result, key, smallest, high):
    index_at = [jax.random.randint(jax.random.fold_in(key, axis), (), 0, length) for axis, length in enumerate(result.shape)]
    longest = result.shape.index(max(result.shape))
    neighbour = index_at[:longest] + [(index_at[longest] + 1) % result.shape[longest]] + index_at[longest + 1:]
    return result.at[tuple(index_at)].set(smallest).at[tuple(neighbour)].set(high)


def shard_levels(rng, shape, cuts, smallest, top_value):
    def one(dim, parts):
        draws = jax.random.uniform(jax.random.fold_in(jax.random.fold_in(rng, 6), dim), (parts,), jnp.float32, smallest / len(cuts), top_value / len(cuts))
        return jnp.repeat(jnp.exp(draws), shape[dim] // parts).reshape((-1,) + (1,) * (len(shape) - dim - 1))

    level = one(*cuts[0])
    for cut in cuts[1:]:
        level = level * one(*cut)
    return level


def shared_out(key, own, number, rows, number_of, top, reach, lean):
    sequence = jax.random.permutation(key, number_of)
    crowded, ordinary = portions_of(number_of, rows * top, reach, lean, True), portions_of(number_of, rows * top, reach, lean, False)
    places = jnp.arange(number_of)

    def named(sizes, turn):
        used = int((sizes > 0).sum())
        fixed = max(1, used // 4)
        passed = fixed + (places - fixed + turn * (used - fixed)) % max(1, number_of - fixed)
        return jnp.zeros((number_of,), jnp.int32).at[sequence[jnp.where(places < fixed, places, passed)]].set(jnp.asarray(sizes, jnp.int32))

    sizes = jnp.where(number % 4 == 0, named(crowded, number // 4), named(ordinary, number - number // 4 - 1))
    mixed = jax.random.permutation(jax.random.fold_in(own, 3), number_of)
    source_of, sink = mixed[0:number_of // 2 * 2:2], mixed[1:number_of // 2 * 2:2]
    margin = jnp.minimum(sizes[source_of] - 1, reach - sizes[sink]) // 2
    margin = jnp.where((source_of == sequence[0]) | (sink == sequence[0]) | (sizes[sink] == 0), 0, jnp.maximum(margin, 0))
    passed = jax.random.randint(jax.random.fold_in(own, 4), (number_of // 2,), 0, 1 << 20) % (margin + 1)
    sizes = sizes.at[source_of].add(-passed).at[sink].add(passed)
    labels = jnp.searchsorted(jnp.cumsum(sizes), jnp.arange(rows * top), side="right").astype(jnp.int32)
    grid = labels.reshape(top, rows).T
    grid = grid[jax.random.permutation(jax.random.fold_in(own, 1), rows)]
    turn = jax.random.randint(jax.random.fold_in(own, 2), (rows, 1), 0, top)
    return jnp.take_along_axis(grid, (jnp.arange(top)[None, :] + turn) % top, axis=1)


def portions_of(count, total, limit, lean, full):
    weights = [(1 << 20) // math.isqrt(rank ** lean) + 1 for rank in range(1, count + 1)]
    largest = limit if full else min(limit, max(-(-total // count), total * weights[0] // sum(weights)))
    least = 1 if total - largest >= count - 1 else 0
    counts, surplus = [largest] + [least] * (count - 1), total - largest - least * (count - 1)
    while surplus > 0:
        free = [i for i in range(1, count) if counts[i] < largest] or [i for i in range(1, count) if counts[i] < limit]
        pool, budget = sum([weights[i] for i in free]), surplus
        for i in free:
            addition = min(limit - counts[i], max(1, budget * weights[i] // pool), surplus)
            counts[i] = counts[i] + addition
            surplus = surplus - addition
    return np.array(counts)


def noise(own_key, extent, deviation, most, shards=(), held_as=jnp.bfloat16):
    level = shard_levels(own_key, extent, shards, -0.22, 0.18) if shards else 1.0
    values = jax.random.normal(own_key, extent, jnp.float32) * deviation * level
    return jnp.minimum(jnp.maximum(values, -most), most).astype(held_as)


def setup_inputs(seed: int = 0) -> dict:
    arg_keys = jax.random.split(jax.random.key(seed), 5)
    radiances = noise(arg_keys[0], (CHAN, OBS), 1.0, 6.0, ((0, 4), (1, 8)), jnp.float32)
    band_keys = jax.random.split(jax.random.fold_in(arg_keys[1], 1), OBS // OBS_DEV)
    band_turns = jax.random.permutation(jax.random.fold_in(arg_keys[1], 3), OBS // OBS_DEV)
    band = jax.vmap(lambda own, number: shared_out(jax.random.fold_in(arg_keys[1], 2), own, number, OBS_DEV, N_ROWS, 1, CAP, 2))(band_keys, band_turns).reshape((OBS, 1))
    row_in_band = touch_ends(jax.random.randint(arg_keys[2], (OBS,), 0, ROWS_DEV), jax.random.fold_in(arg_keys[2], 1), 0, ROWS_DEV - 1).astype(jnp.int32)
    column = touch_ends(jax.random.randint(arg_keys[3], (OBS,), 0, COLS), jax.random.fold_in(arg_keys[3], 1), 0, COLS - 1).astype(jnp.int32)
    return {"radiances": radiances, "band": band, "row_in_band": row_in_band, "column": column}


def reference(radiances, band, row_in_band, column):
    lat = band[:, 0] * ROWS_DEV + row_in_band
    cell = (lat * COLS + column).astype(jnp.int32)
    cells = LATS * COLS
    ones = jnp.ones(cell.shape, jnp.float32)
    count = jax.ops.segment_sum(ones, cell, num_segments=cells)
    values = radiances.astype(jnp.float32).T
    first = jax.ops.segment_sum(values, cell, num_segments=cells)
    second = jax.ops.segment_sum(values * values, cell, num_segments=cells)
    denom = jnp.maximum(count, 1.0)[:, None]
    mean = first / denom
    var = jnp.maximum(second / denom - mean * mean, 0.0)
    spread = lax.optimization_barrier(jnp.sum(var, axis=1))
    scale = lax.rsqrt(1.0 + spread / CHAN)
    departure = (radiances - mean[cell].T) * scale[cell][None, :]
    cell_count = count.reshape(LATS, COLS).astype(jnp.int32)
    cell_mean = mean.T.reshape(CHAN, LATS, COLS)
    cell_var = var.T.reshape(CHAN, LATS, COLS)
    return (cell_count, cell_mean, cell_var, spread.reshape(LATS, COLS), departure)
```

```python
import functools

import jax
import jax.numpy as jnp
from jax import lax
from jax.experimental import pallas as pl
from jax.experimental.pallas import tpu as pltpu
from jax.sharding import PartitionSpec as P

CHAN = 16
COLS = 1440
ROWS_DEV = 4
LOW = 256
BLOCKS = -(-COLS // LOW)
QS = BLOCKS * ROWS_DEV
F32 = jnp.float32
BF16 = jnp.bfloat16
MESH = pl.DeviceIdType.MESH
NT = (((1,), (1,)), ((), ()))
NN = (((1,), (0,)), ((), ()))


def iota(shape, axis):
    return lax.broadcasted_iota(jnp.int32, shape, axis)


def onehot(mask):
    return jnp.where(mask, 1.0, 0.0)


def two(values):
    high = values.astype(BF16).astype(F32)
    return high, values - high


def dot(a, b, dims):
    return lax.dot_general(a, b, dims, preferred_element_type=F32)


def rank_of(dest, nrows):
    obs = dest.shape[1]
    nblock = obs // 128
    hot = onehot(iota((nrows, obs), 0) == dest)
    stacked = jnp.concatenate([hot[:, b * 128 : (b + 1) * 128] for b in range(nblock)], axis=0)
    stacked_b = stacked.astype(BF16)
    size = nblock * nrows
    upper = onehot(iota((128, 128), 0) <= iota((128, 128), 1)).astype(BF16)
    inner = dot(stacked_b, upper, NN)
    r, c = iota((size, size), 0), iota((size, size), 1)
    earlier = onehot((c < r) & (lax.rem(r - c + size, nrows) == 0)).astype(BF16)
    before = jnp.sum(dot(earlier, stacked_b, NN), axis=1, keepdims=True)
    ranks = stacked * (inner + before)
    rows = [
        jnp.sum(ranks[b * nrows : (b + 1) * nrows], axis=0, keepdims=True) for b in range(nblock)
    ]
    return (jnp.concatenate(rows, axis=1) - 1.0).astype(jnp.int32)


def spill(out, values):
    for j in range(BLOCKS):
        start = j * LOW
        width = min(LOW, COLS - start)
        out[:, start : start + width] = values[j * ROWS_DEV : (j + 1) * ROWS_DEV, :width].astype(
            out.dtype
        )


def kernel(
    nrows,
    nchan,
    rad_ref,
    band_ref,
    rib_ref,
    col_ref,
    cnt_out,
    mean_out,
    var_out,
    spr_out,
    dep_out,
    rank_hot,
    col_hot,
    q_hot,
    acc,
    send_v,
    send_c,
    recv_v,
    recv_c,
    parts,
    back_s,
    back_r,
    sv,
    rv,
    sc,
    rc,
    sp,
    rp,
    sb,
    rb,
):
    me = lax.axis_index("rows")
    mc = lax.axis_index("chan")
    fields, obs = rad_ref.shape
    cap = rank_hot.shape[0]

    barrier = pltpu.get_barrier_semaphore()
    for d in range(1, nrows):
        pl.semaphore_signal(
            barrier, inc=1, device_id={"rows": lax.rem(me + d, nrows)}, device_id_type=MESH
        )
    for d in range(1, nchan):
        pl.semaphore_signal(
            barrier, inc=1, device_id={"chan": lax.rem(mc + d, nchan)}, device_id_type=MESH
        )

    dest = band_ref[...]
    rank = rank_of(dest, nrows)
    rank_hot[...] = onehot(iota((cap, obs), 0) == rank).astype(BF16)
    rad = rad_ref[...]
    high, rest = two(rad)
    middle, low = two(rest)
    col = col_ref[...]
    code = (col // LOW) * ROWS_DEV + rib_ref[...] + 1
    pad = -(3 * fields + 2) % 8
    group = 3 * fields + 2 + pad
    payload = jnp.concatenate(
        [high, middle, low, code.astype(F32), (col % LOW).astype(F32), jnp.zeros((pad, obs), F32)],
        axis=0,
    )
    left = jnp.concatenate(
        [jnp.where(dest == lax.rem(me + d, nrows), payload, 0.0) for d in range(nrows)], axis=0
    ).astype(BF16)
    placed = dot(left, rank_hot[...], NT)
    pl.semaphore_wait(barrier, nrows - 1 + nchan - 1)

    out_copies = []
    for d in list(range(1, nrows)) + [0]:
        part = placed[d * group : (d + 1) * group]
        values = (part[:fields] + part[fields : 2 * fields]) + part[2 * fields : 3 * fields]
        cells = part[3 * fields : 3 * fields + 1] * LOW + part[3 * fields + 1 : 3 * fields + 2]
        if d == 0:
            recv_v[0] = values
            recv_c[0] = cells
            continue
        send_v[d] = values
        send_c[d] = cells
        to = {"rows": lax.rem(me + d, nrows)}
        for src, dst, s, r in ((send_v, recv_v, sv, rv), (send_c, recv_c, sc, rc)):
            copy = pltpu.make_async_remote_copy(
                src_ref=src.at[d],
                dst_ref=dst.at[d],
                send_sem=s.at[d],
                recv_sem=r.at[d],
                device_id=to,
                device_id_type=MESH,
            )
            copy.start()
            out_copies.append(copy)

    for d in range(nrows):
        if d > 0:
            out_copies[2 * d - 2].wait_recv()
            out_copies[2 * d - 1].wait_recv()
        values = recv_v[d]
        cells = recv_c[d].astype(jnp.int32)
        cols_t = onehot(iota((LOW, cap), 0) == (cells & (LOW - 1))).astype(BF16)
        col_hot[d] = cols_t
        quads = onehot(iota((QS, cap), 0) == (cells // LOW) - 1)
        q_hot[d] = quads
        features = two(values) + two(values * values)
        rows = [quads] + [quads * x[f : f + 1] for x in features for f in range(fields)]
        sums = dot(jnp.concatenate(rows, axis=0).astype(BF16), cols_t, NT)
        if d == 0:
            acc[...] = sums
        else:
            acc[...] += sums

    count = acc[0:QS]
    inverse = 1.0 / jnp.maximum(count, 1.0)
    means, variances = [], []
    for f in range(fields):

        def total(k):
            at = (1 + k * fields + f) * QS
            after = at + fields * QS
            return acc[at : at + QS] + acc[after : after + QS]

        mean = total(0) * inverse
        means.append(mean)
        variances.append(jnp.maximum(total(2) * inverse - mean * mean, 0.0))
    partial = variances[0]
    for f in range(1, fields):
        partial = partial + variances[f]
    parts[mc] = partial
    part_copies = []
    for d in range(1, nchan):
        copy = pltpu.make_async_remote_copy(
            src_ref=parts.at[mc],
            dst_ref=parts.at[mc],
            send_sem=sp.at[d],
            recv_sem=rp.at[d],
            device_id={"chan": lax.rem(mc + d, nchan)},
            device_id_type=MESH,
        )
        copy.start()
        part_copies.append(copy)

    spill(cnt_out, count)
    for f in range(fields):
        spill(mean_out.at[f], means[f])
        spill(var_out.at[f], variances[f])
    split = [two(mean) for mean in means]
    table = jnp.concatenate([x[0] for x in split] + [x[1] for x in split], axis=0).astype(BF16)
    for d in range(nrows):
        picked = dot(table, col_hot[d], NN)
        quads = q_hot[d]
        found = []
        for f in range(fields):
            at = (fields + f) * QS
            both = picked[f * QS : (f + 1) * QS] + picked[at : at + QS]
            found.append(jnp.sum(both * quads, axis=0, keepdims=True))
        back_s[d] = recv_v[d] - jnp.concatenate(found, axis=0)

    for copy in part_copies:
        copy.wait_recv()
    spread = parts[0]
    for c in range(1, nchan):
        spread = spread + parts[c]
    scale = lax.rsqrt(1.0 + spread / CHAN)
    table = jnp.concatenate(two(scale), axis=0).astype(BF16)
    back_copies = []
    for d in list(range(1, nrows)) + [0]:
        picked = dot(table, col_hot[d], NN)
        found = jnp.sum((picked[:QS] + picked[QS:]) * q_hot[d], axis=0, keepdims=True)
        shifted = back_s[d] * found
        if d == 0:
            back_r[0] = shifted
            continue
        back_s[d] = shifted
        copy = pltpu.make_async_remote_copy(
            src_ref=back_s.at[d],
            dst_ref=back_r.at[d],
            send_sem=sb.at[d],
            recv_sem=rb.at[d],
            device_id={"rows": lax.rem(me + nrows - d, nrows)},
            device_id_type=MESH,
        )
        copy.start()
        back_copies.append(copy)
    spill(spr_out, spread)

    for copy in back_copies:
        copy.wait_recv()
    returned = jnp.concatenate([back_r[d] for d in range(nrows)], axis=0)
    size = nrows * fields
    both = dot(jnp.concatenate(two(returned), axis=0).astype(BF16), rank_hot[...], NN)
    merged = both[:size] + both[size:]
    per = max(1, 8 // fields)
    inside = jnp.zeros((per * fields, 1), jnp.int32)
    for j in range(1, per):
        inside = inside + (iota((per * fields, 1), 0) >= j * fields).astype(jnp.int32)
    result = None
    for p in range(nrows // per):
        owner = lax.rem(me + p * per + inside, nrows)
        block = merged[p * per * fields : (p + 1) * per * fields]
        term = jnp.where(dest == owner, block, 0.0)
        result = term if result is None else result + term
    final = result[:fields]
    for j in range(1, per):
        final = final + result[j * fields : (j + 1) * fields]
    dep_out[...] = final

    for copy in out_copies + part_copies + back_copies:
        copy.wait_send()


def body(radiances, band, row_in_band, column):
    nrows = lax.axis_size("rows")
    nchan = lax.axis_size("chan")
    fields, obs = radiances.shape
    cap = 2 * obs // nrows
    nfeat = 1 + 4 * fields
    vmem = pl.BlockSpec(memory_space=pltpu.VMEM)
    dma = pltpu.SemaphoreType.DMA
    return pl.pallas_call(
        functools.partial(kernel, nrows, nchan),
        out_shape=(
            jax.ShapeDtypeStruct((ROWS_DEV, COLS), jnp.int32),
            jax.ShapeDtypeStruct((fields, ROWS_DEV, COLS), F32),
            jax.ShapeDtypeStruct((fields, ROWS_DEV, COLS), F32),
            jax.ShapeDtypeStruct((ROWS_DEV, COLS), F32),
            jax.ShapeDtypeStruct((fields, obs), F32),
        ),
        in_specs=[vmem] * 4,
        out_specs=(vmem,) * 5,
        scratch_shapes=[
            pltpu.VMEM((cap, obs), BF16),
            pltpu.VMEM((nrows, LOW, cap), BF16),
            pltpu.VMEM((nrows, QS, cap), F32),
            pltpu.VMEM((nfeat * QS, LOW), F32),
            pltpu.VMEM((nrows, fields, cap), F32),
            pltpu.VMEM((nrows, 1, cap), F32),
            pltpu.VMEM((nrows, fields, cap), F32),
            pltpu.VMEM((nrows, 1, cap), F32),
            pltpu.VMEM((nchan, QS, LOW), F32),
            pltpu.VMEM((nrows, fields, cap), F32),
            pltpu.VMEM((nrows, fields, cap), F32),
            dma((nrows,)),
            dma((nrows,)),
            dma((nrows,)),
            dma((nrows,)),
            dma((nchan,)),
            dma((nchan,)),
            dma((nrows,)),
            dma((nrows,)),
        ],
        compiler_params=pltpu.CompilerParams(collective_id=0, has_side_effects=True),
    )(
        radiances,
        band.reshape(1, obs),
        row_in_band.reshape(1, obs),
        column.reshape(1, obs),
    )


def solution(mesh):
    in_specs = (P("chan", "rows"), P("rows", None), P("rows"), P("rows"))
    out_specs = (
        P("rows", None),
        P("chan", "rows", None),
        P("chan", "rows", None),
        P("rows", None),
        P("chan", "rows"),
    )
    return jax.shard_map(body, mesh=mesh, in_specs=in_specs, out_specs=out_specs, check_vma=False)
```

```python
import functools

import jax
import jax.numpy as jnp
from jax import lax
from jax.experimental import pallas as pl
from jax.experimental.pallas import tpu as pltpu
from jax.sharding import PartitionSpec as P

CHAN = 16
COLS = 1440
ROWS_DEV = 4
LOW = 256
BLOCKS = -(-COLS // LOW)
QS = BLOCKS * ROWS_DEV
F32 = jnp.float32
BF16 = jnp.bfloat16
MESH = pl.DeviceIdType.MESH
NT = (((1,), (1,)), ((), ()))
NN = (((1,), (0,)), ((), ()))


def iota(shape, axis):
    return lax.broadcasted_iota(jnp.int32, shape, axis)


def onehot(mask):
    return jnp.where(mask, 1.0, 0.0)


def two(values):
    high = values.astype(BF16).astype(F32)
    return high, values - high


def dot(a, b, dims):
    return lax.dot_general(a, b, dims, preferred_element_type=F32)


def rank_of(dest, nrows):
    obs = dest.shape[1]
    nblock = obs // 128
    hot = onehot(iota((nrows, obs), 0) == dest)
    stacked = jnp.concatenate([hot[:, b * 128 : (b + 1) * 128] for b in range(nblock)], axis=0)
    stacked_b = stacked.astype(BF16)
    size = nblock * nrows
    upper = onehot(iota((128, 128), 0) <= iota((128, 128), 1)).astype(BF16)
    inner = dot(stacked_b, upper, NN)
    r, c = iota((size, size), 0), iota((size, size), 1)
    earlier = onehot((c < r) & (lax.rem(r - c + size, nrows) == 0)).astype(BF16)
    before = jnp.sum(dot(earlier, stacked_b, NN), axis=1, keepdims=True)
    ranks = stacked * (inner + before)
    rows = [
        jnp.sum(ranks[b * nrows : (b + 1) * nrows], axis=0, keepdims=True) for b in range(nblock)
    ]
    return (jnp.concatenate(rows, axis=1) - 1.0).astype(jnp.int32)


def spill(out, values):
    for j in range(BLOCKS):
        start = j * LOW
        width = min(LOW, COLS - start)
        out[:, start : start + width] = values[j * ROWS_DEV : (j + 1) * ROWS_DEV, :width].astype(
            out.dtype
        )


def unplace(me, nrows, fields, returned, rank_hot, dest):
    size = nrows * fields
    both = dot(jnp.concatenate(two(returned), axis=0).astype(BF16), rank_hot[...], NN)
    merged = both[:size] + both[size:]
    per = max(1, 8 // fields)
    inside = jnp.zeros((per * fields, 1), jnp.int32)
    for j in range(1, per):
        inside = inside + (iota((per * fields, 1), 0) >= j * fields).astype(jnp.int32)
    result = None
    for p in range(nrows // per):
        owner = lax.rem(me + p * per + inside, nrows)
        block = merged[p * per * fields : (p + 1) * per * fields]
        term = jnp.where(dest == owner, block, 0.0)
        result = term if result is None else result + term
    final = result[:fields]
    for j in range(1, per):
        final = final + result[j * fields : (j + 1) * fields]
    return final


def kernel(
    nrows,
    nchan,
    rad_in,
    band_in,
    rib_in,
    col_in,
    cnt_out,
    mean_out,
    var_out,
    spr_out,
    diff_out,
    scale_out,
    rank_hot,
    dest_out,
    rad_ref,
    band_ref,
    rib_ref,
    col_ref,
    col_hot,
    q_hot,
    acc,
    send_v,
    send_c,
    recv_v,
    recv_c,
    parts,
    back_s,
    back_r,
    scale_s,
    scale_r,
    ins,
    sv,
    rv,
    sc,
    rc,
    sp,
    rp,
    sb,
    rb,
    ss,
    rs,
):
    me = lax.axis_index("rows")
    mc = lax.axis_index("chan")
    fields, obs = rad_ref.shape
    cap = rank_hot.shape[0]

    fetches = [
        pltpu.make_async_copy(a, b, ins.at[i])
        for i, (a, b) in enumerate(
            ((band_in, band_ref), (rad_in, rad_ref), (rib_in, rib_ref), (col_in, col_ref))
        )
    ]
    for fetch in fetches:
        fetch.start()
    barrier = pltpu.get_barrier_semaphore()
    for d in range(1, nrows):
        pl.semaphore_signal(
            barrier, inc=1, device_id={"rows": lax.rem(me + d, nrows)}, device_id_type=MESH
        )
    for d in range(1, nchan):
        pl.semaphore_signal(
            barrier, inc=1, device_id={"chan": lax.rem(mc + d, nchan)}, device_id_type=MESH
        )

    fetches[0].wait()
    dest = band_ref[...]
    dest_out[...] = dest
    rank = rank_of(dest, nrows)
    rank_hot[...] = onehot(iota((cap, obs), 0) == rank).astype(BF16)
    for fetch in fetches[1:]:
        fetch.wait()
    rad = rad_ref[...]
    high, rest = two(rad)
    middle, low = two(rest)
    col = col_ref[...]
    code = (col // LOW) * ROWS_DEV + rib_ref[...] + 1
    pad = -(3 * fields + 2) % 8
    group = 3 * fields + 2 + pad
    payload = jnp.concatenate(
        [high, middle, low, code.astype(F32), (col % LOW).astype(F32), jnp.zeros((pad, obs), F32)],
        axis=0,
    )
    left = jnp.concatenate(
        [jnp.where(dest == lax.rem(me + d, nrows), payload, 0.0) for d in range(nrows)], axis=0
    ).astype(BF16)
    placed = dot(left, rank_hot[...], NT)
    pl.semaphore_wait(barrier, nrows - 1 + nchan - 1)

    out_copies = []
    for d in list(range(1, nrows)) + [0]:
        part = placed[d * group : (d + 1) * group]
        values = (part[:fields] + part[fields : 2 * fields]) + part[2 * fields : 3 * fields]
        cells = part[3 * fields : 3 * fields + 1] * LOW + part[3 * fields + 1 : 3 * fields + 2]
        if d == 0:
            recv_v[0] = values
            recv_c[0] = cells
            continue
        send_v[d] = values
        send_c[d] = cells
        to = {"rows": lax.rem(me + d, nrows)}
        for src, dst, s, r in ((send_v, recv_v, sv, rv), (send_c, recv_c, sc, rc)):
            copy = pltpu.make_async_remote_copy(
                src_ref=src.at[d],
                dst_ref=dst.at[d],
                send_sem=s.at[d],
                recv_sem=r.at[d],
                device_id=to,
                device_id_type=MESH,
            )
            copy.start()
            out_copies.append(copy)

    for d in range(nrows):
        if d > 0:
            out_copies[2 * d - 2].wait_recv()
            out_copies[2 * d - 1].wait_recv()
        values = recv_v[d]
        cells = recv_c[d].astype(jnp.int32)
        cols_t = onehot(iota((LOW, cap), 0) == (cells & (LOW - 1))).astype(BF16)
        col_hot[d] = cols_t
        quads = onehot(iota((QS, cap), 0) == (cells // LOW) - 1)
        q_hot[d] = quads
        features = two(values) + two(values * values)
        rows = [quads] + [quads * x[f : f + 1] for x in features for f in range(fields)]
        sums = dot(jnp.concatenate(rows, axis=0).astype(BF16), cols_t, NT)
        if d == 0:
            acc[...] = sums
        else:
            acc[...] += sums

    count = acc[0:QS]
    inverse = 1.0 / jnp.maximum(count, 1.0)
    means, variances = [], []
    for f in range(fields):

        def total(k):
            at = (1 + k * fields + f) * QS
            after = at + fields * QS
            return acc[at : at + QS] + acc[after : after + QS]

        mean = total(0) * inverse
        means.append(mean)
        variances.append(jnp.maximum(total(2) * inverse - mean * mean, 0.0))
    partial = variances[0]
    for f in range(1, fields):
        partial = partial + variances[f]
    parts[mc] = partial
    part_copies = []
    for d in range(1, nchan):
        copy = pltpu.make_async_remote_copy(
            src_ref=parts.at[mc],
            dst_ref=parts.at[mc],
            send_sem=sp.at[d],
            recv_sem=rp.at[d],
            device_id={"chan": lax.rem(mc + d, nchan)},
            device_id_type=MESH,
        )
        copy.start()
        part_copies.append(copy)

    split = [two(mean) for mean in means]
    table = jnp.concatenate([x[0] for x in split] + [x[1] for x in split], axis=0).astype(BF16)
    back_copies = []
    for d in list(range(1, nrows)) + [0]:
        picked = dot(table, col_hot[d], NN)
        quads = q_hot[d]
        found = []
        for f in range(fields):
            at = (fields + f) * QS
            both = picked[f * QS : (f + 1) * QS] + picked[at : at + QS]
            found.append(jnp.sum(both * quads, axis=0, keepdims=True))
        diff = recv_v[d] - jnp.concatenate(found, axis=0)
        if d == 0:
            back_r[0] = diff
            continue
        back_s[d] = diff
        copy = pltpu.make_async_remote_copy(
            src_ref=back_s.at[d],
            dst_ref=back_r.at[d],
            send_sem=sb.at[d],
            recv_sem=rb.at[d],
            device_id={"rows": lax.rem(me + nrows - d, nrows)},
            device_id_type=MESH,
        )
        copy.start()
        back_copies.append(copy)

    for copy in part_copies:
        copy.wait_recv()
    spread = parts[0]
    for c in range(1, nchan):
        spread = spread + parts[c]
    scale = lax.rsqrt(1.0 + spread / CHAN)
    table = jnp.concatenate(two(scale), axis=0).astype(BF16)
    scale_copies = []
    for d in list(range(1, nrows)) + [0]:
        picked = dot(table, col_hot[d], NN)
        found = jnp.sum((picked[:QS] + picked[QS:]) * q_hot[d], axis=0, keepdims=True)
        if d == 0:
            scale_r[0] = found
            continue
        scale_s[d] = found
        copy = pltpu.make_async_remote_copy(
            src_ref=scale_s.at[d],
            dst_ref=scale_r.at[d],
            send_sem=ss.at[d],
            recv_sem=rs.at[d],
            device_id={"rows": lax.rem(me + nrows - d, nrows)},
            device_id_type=MESH,
        )
        copy.start()
        scale_copies.append(copy)
    spill(spr_out, spread)
    spill(cnt_out, count)
    for f in range(fields):
        spill(mean_out.at[f], means[f])
        spill(var_out.at[f], variances[f])

    for copy in back_copies:
        copy.wait_recv()
    returned = jnp.concatenate([back_r[d] for d in range(nrows)], axis=0)
    diff_out[...] = unplace(me, nrows, fields, returned, rank_hot, dest)
    for copy in scale_copies:
        copy.wait_recv()
    scale_out[...] = jnp.concatenate([scale_r[d] for d in range(nrows)], axis=0)

    for copy in out_copies + part_copies + back_copies + scale_copies:
        copy.wait_send()


def finish(
    nrows,
    cnt_ref,
    mean_ref,
    var_ref,
    spr_ref,
    diff_ref,
    scale_ref,
    rank_hot,
    band_ref,
    cnt_out,
    mean_out,
    var_out,
    spr_out,
    dep_out,
    sems,
):
    pairs = ((mean_ref, mean_out), (var_ref, var_out), (cnt_ref, cnt_out), (spr_ref, spr_out))
    copies = [pltpu.make_async_copy(a, b, sems.at[i]) for i, (a, b) in enumerate(pairs)]
    for copy in copies:
        copy.start()
    me = lax.axis_index("rows")
    both = dot(jnp.concatenate(two(scale_ref[...]), axis=0).astype(BF16), rank_hot[...], NN)
    merged = both[:nrows] + both[nrows:]
    owner = lax.rem(me + iota((nrows, 1), 0), nrows)
    mine = jnp.where(band_ref[...] == owner, merged, 0.0)
    dep_out[...] = diff_ref[...] * jnp.sum(mine, axis=0, keepdims=True)
    for copy in copies:
        copy.wait()


def body(radiances, band, row_in_band, column):
    nrows = lax.axis_size("rows")
    nchan = lax.axis_size("chan")
    fields, obs = radiances.shape
    cap = 2 * obs // nrows
    nfeat = 1 + 4 * fields
    vmem = pl.BlockSpec(memory_space=pltpu.VMEM)
    anywhere = pl.BlockSpec(memory_space=pl.ANY)
    dma = pltpu.SemaphoreType.DMA
    band = band.reshape(1, obs)
    shapes = (
        ((ROWS_DEV, COLS), jnp.int32),
        ((fields, ROWS_DEV, COLS), F32),
        ((fields, ROWS_DEV, COLS), F32),
        ((ROWS_DEV, COLS), F32),
    )
    held = pl.pallas_call(
        functools.partial(kernel, nrows, nchan),
        out_shape=tuple(pltpu.VMEM(s, t) for s, t in shapes)
        + (
            pltpu.VMEM((fields, obs), F32),
            pltpu.VMEM((nrows, cap), F32),
            pltpu.VMEM((cap, obs), BF16),
            pltpu.VMEM((1, obs), jnp.int32),
        ),
        in_specs=[pl.BlockSpec(memory_space=pltpu.HBM)] * 4,
        out_specs=(vmem,) * 8,
        scratch_shapes=[
            pltpu.VMEM((fields, obs), F32),
            pltpu.VMEM((1, obs), jnp.int32),
            pltpu.VMEM((1, obs), jnp.int32),
            pltpu.VMEM((1, obs), jnp.int32),
            pltpu.VMEM((nrows, LOW, cap), BF16),
            pltpu.VMEM((nrows, QS, cap), F32),
            pltpu.VMEM((nfeat * QS, LOW), F32),
            pltpu.VMEM((nrows, fields, cap), F32),
            pltpu.VMEM((nrows, 1, cap), F32),
            pltpu.VMEM((nrows, fields, cap), F32),
            pltpu.VMEM((nrows, 1, cap), F32),
            pltpu.VMEM((nchan, QS, LOW), F32),
            pltpu.VMEM((nrows, fields, cap), F32),
            pltpu.VMEM((nrows, fields, cap), F32),
            pltpu.VMEM((nrows, 1, cap), F32),
            pltpu.VMEM((nrows, 1, cap), F32),
            dma((4,)),
            dma((nrows,)),
            dma((nrows,)),
            dma((nrows,)),
            dma((nrows,)),
            dma((nchan,)),
            dma((nchan,)),
            dma((nrows,)),
            dma((nrows,)),
            dma((nrows,)),
            dma((nrows,)),
        ],
        compiler_params=pltpu.CompilerParams(
            collective_id=0, has_side_effects=True, vmem_limit_bytes=32 * 1024 * 1024
        ),
    )(
        *(
            pltpu.with_memory_space_constraint(x, pltpu.HBM)
            for x in (radiances, band, row_in_band.reshape(1, obs), column.reshape(1, obs))
        )
    )
    return pl.pallas_call(
        functools.partial(finish, nrows),
        out_shape=tuple(jax.ShapeDtypeStruct(s, t) for s, t in shapes)
        + (jax.ShapeDtypeStruct((fields, obs), F32),),
        in_specs=[vmem] * 8,
        out_specs=(anywhere,) * 4 + (vmem,),
        scratch_shapes=[dma((4,))],
        compiler_params=pltpu.CompilerParams(vmem_limit_bytes=32 * 1024 * 1024),
    )(*held)


def solution(mesh):
    in_specs = (P("chan", "rows"), P("rows", None), P("rows"), P("rows"))
    out_specs = (
        P("rows", None),
        P("chan", "rows", None),
        P("chan", "rows", None),
        P("rows", None),
        P("chan", "rows"),
    )
    return jax.shard_map(body, mesh=mesh, in_specs=in_specs, out_specs=out_specs, check_vma=False)
```

```python
import functools

import jax
import jax.numpy as jnp
from jax import lax
from jax.experimental import pallas as pl
from jax.experimental.pallas import tpu as pltpu
from jax.sharding import PartitionSpec as P

CHAN = 16
COLS = 1440
ROWS_DEV = 4
LOW = 256
BLOCKS = -(-COLS // LOW)
QS = BLOCKS * ROWS_DEV
F32 = jnp.float32
BF16 = jnp.bfloat16
MESH = pl.DeviceIdType.MESH
NT = (((1,), (1,)), ((), ()))
NN = (((1,), (0,)), ((), ()))


def iota(shape, axis):
    return lax.broadcasted_iota(jnp.int32, shape, axis)


def onehot(mask):
    return jnp.where(mask, 1.0, 0.0)


def two(values):
    high = values.astype(BF16).astype(F32)
    return high, values - high


def dot(a, b, dims):
    return lax.dot_general(a, b, dims, preferred_element_type=F32)


def rank_of(dest, nrows):
    obs = dest.shape[1]
    nblock = obs // 128
    hot = onehot(iota((nrows, obs), 0) == dest)
    stacked = jnp.concatenate([hot[:, b * 128 : (b + 1) * 128] for b in range(nblock)], axis=0)
    stacked_b = stacked.astype(BF16)
    size = nblock * nrows
    upper = onehot(iota((128, 128), 0) <= iota((128, 128), 1)).astype(BF16)
    inner = dot(stacked_b, upper, NN)
    r, c = iota((size, size), 0), iota((size, size), 1)
    earlier = onehot((c < r) & (lax.rem(r - c + size, nrows) == 0)).astype(BF16)
    before = jnp.sum(dot(earlier, stacked_b, NN), axis=1, keepdims=True)
    ranks = stacked * (inner + before)
    rows = [
        jnp.sum(ranks[b * nrows : (b + 1) * nrows], axis=0, keepdims=True) for b in range(nblock)
    ]
    return (jnp.concatenate(rows, axis=1) - 1.0).astype(jnp.int32)


def spill(out, values):
    for j in range(BLOCKS):
        start = j * LOW
        width = min(LOW, COLS - start)
        out[:, start : start + width] = values[j * ROWS_DEV : (j + 1) * ROWS_DEV, :width].astype(
            out.dtype
        )


def unplace(me, nrows, fields, returned, rank_hot, dest):
    size = nrows * fields
    both = dot(jnp.concatenate(two(returned), axis=0).astype(BF16), rank_hot[...], NN)
    merged = both[:size] + both[size:]
    per = max(1, 8 // fields)
    inside = jnp.zeros((per * fields, 1), jnp.int32)
    for j in range(1, per):
        inside = inside + (iota((per * fields, 1), 0) >= j * fields).astype(jnp.int32)
    result = None
    for p in range(nrows // per):
        owner = lax.rem(me + p * per + inside, nrows)
        block = merged[p * per * fields : (p + 1) * per * fields]
        term = jnp.where(dest == owner, block, 0.0)
        result = term if result is None else result + term
    final = result[:fields]
    for j in range(1, per):
        final = final + result[j * fields : (j + 1) * fields]
    return final


def kernel(
    nrows,
    nchan,
    rad_in,
    band_in,
    rib_in,
    col_in,
    cnt_out,
    mean_out,
    var_out,
    spr_out,
    diff_out,
    scale_out,
    rank_hot,
    dest_out,
    rad_ref,
    band_ref,
    rib_ref,
    col_ref,
    col_hot,
    q_hot,
    acc,
    send_v,
    send_c,
    recv_v,
    recv_c,
    parts,
    back_s,
    back_r,
    scale_s,
    scale_r,
    ins,
    sv,
    rv,
    sc,
    rc,
    sp,
    rp,
    sb,
    rb,
    ss,
    rs,
):
    me = lax.axis_index("rows")
    mc = lax.axis_index("chan")
    fields, obs = rad_ref.shape
    cap = rank_hot.shape[0]

    fetches = [
        pltpu.make_async_copy(a, b, ins.at[i])
        for i, (a, b) in enumerate(
            ((band_in, band_ref), (rad_in, rad_ref), (rib_in, rib_ref), (col_in, col_ref))
        )
    ]
    for fetch in fetches:
        fetch.start()
    barrier = pltpu.get_barrier_semaphore()
    for d in range(nrows):
        for e in range(nchan):
            if d + e > 0:
                to = {"rows": lax.rem(me + d, nrows), "chan": lax.rem(mc + e, nchan)}
                pl.semaphore_signal(barrier, inc=1, device_id=to, device_id_type=MESH)

    fetches[0].wait()
    dest = band_ref[...]
    dest_out[...] = dest
    rank = rank_of(dest, nrows)
    rank_hot[...] = onehot(iota((cap, obs), 0) == rank).astype(BF16)
    for fetch in fetches[1:]:
        fetch.wait()
    rad = rad_ref[...]
    high, rest = two(rad)
    middle, low = two(rest)
    col = col_ref[...]
    code = (col // LOW) * ROWS_DEV + rib_ref[...] + 1
    pad = -(3 * fields + 2) % 8
    group = 3 * fields + 2 + pad
    payload = jnp.concatenate(
        [high, middle, low, code.astype(F32), (col % LOW).astype(F32), jnp.zeros((pad, obs), F32)],
        axis=0,
    )
    left = jnp.concatenate(
        [jnp.where(dest == lax.rem(me + d, nrows), payload, 0.0) for d in range(nrows)], axis=0
    ).astype(BF16)
    placed = dot(left, rank_hot[...], NT)
    pl.semaphore_wait(barrier, nrows * nchan - 1)

    out_copies = []
    for d in list(range(1, nrows)) + [0]:
        part = placed[d * group : (d + 1) * group]
        values = (part[:fields] + part[fields : 2 * fields]) + part[2 * fields : 3 * fields]
        cells = part[3 * fields : 3 * fields + 1] * LOW + part[3 * fields + 1 : 3 * fields + 2]
        if d == 0:
            recv_v[0] = values
            recv_c[0] = cells
            continue
        send_v[d] = values
        send_c[d] = cells
        to = {"rows": lax.rem(me + d, nrows)}
        for src, dst, s, r in ((send_v, recv_v, sv, rv), (send_c, recv_c, sc, rc)):
            copy = pltpu.make_async_remote_copy(
                src_ref=src.at[d],
                dst_ref=dst.at[d],
                send_sem=s.at[d],
                recv_sem=r.at[d],
                device_id=to,
                device_id_type=MESH,
            )
            copy.start()
            out_copies.append(copy)

    for d in range(nrows):
        if d > 0:
            out_copies[2 * d - 2].wait_recv()
            out_copies[2 * d - 1].wait_recv()
        values = recv_v[d]
        cells = recv_c[d].astype(jnp.int32)
        cols_t = onehot(iota((LOW, cap), 0) == (cells & (LOW - 1))).astype(BF16)
        col_hot[d] = cols_t
        quads = onehot(iota((QS, cap), 0) == (cells // LOW) - 1)
        q_hot[d] = quads
        features = two(values) + two(values * values)
        rows = [quads] + [quads * x[f : f + 1] for x in features for f in range(fields)]
        sums = dot(jnp.concatenate(rows, axis=0).astype(BF16), cols_t, NT)
        if d == 0:
            acc[...] = sums
        else:
            acc[...] += sums

    count = acc[0:QS]
    inverse = 1.0 / jnp.maximum(count, 1.0)
    means, variances = [], []
    for f in range(fields):

        def total(k):
            at = (1 + k * fields + f) * QS
            after = at + fields * QS
            return acc[at : at + QS] + acc[after : after + QS]

        mean = total(0) * inverse
        means.append(mean)
        variances.append(jnp.maximum(total(2) * inverse - mean * mean, 0.0))
    partial = variances[0]
    for f in range(1, fields):
        partial = partial + variances[f]
    table = jnp.concatenate(two(partial), axis=0).astype(BF16)
    scale_copies = []
    for d in list(range(1, nrows)) + [0]:
        picked = dot(table, col_hot[d], NN)
        found = jnp.sum((picked[:QS] + picked[QS:]) * q_hot[d], axis=0, keepdims=True)
        scale_s[d] = found
        if d == 0:
            scale_r[0] = found
        for e in range(nchan):
            if d + e == 0:
                continue
            slot = e * nrows + d
            copy = pltpu.make_async_remote_copy(
                src_ref=scale_s.at[d],
                dst_ref=scale_r.at[slot],
                send_sem=ss.at[slot],
                recv_sem=rs.at[slot],
                device_id={
                    "rows": lax.rem(me + nrows - d, nrows),
                    "chan": lax.rem(mc + e, nchan),
                },
                device_id_type=MESH,
            )
            copy.start()
            scale_copies.append(copy)
    split = [two(mean) for mean in means]
    table = jnp.concatenate([x[0] for x in split] + [x[1] for x in split], axis=0).astype(BF16)
    back_copies = []
    for d in list(range(1, nrows)) + [0]:
        picked = dot(table, col_hot[d], NN)
        quads = q_hot[d]
        found = []
        for f in range(fields):
            at = (fields + f) * QS
            both = picked[f * QS : (f + 1) * QS] + picked[at : at + QS]
            found.append(jnp.sum(both * quads, axis=0, keepdims=True))
        diff = recv_v[d] - jnp.concatenate(found, axis=0)
        if d == 0:
            back_r[0] = diff
            continue
        back_s[d] = diff
        copy = pltpu.make_async_remote_copy(
            src_ref=back_s.at[d],
            dst_ref=back_r.at[d],
            send_sem=sb.at[d],
            recv_sem=rb.at[d],
            device_id={"rows": lax.rem(me + nrows - d, nrows)},
            device_id_type=MESH,
        )
        copy.start()
        back_copies.append(copy)

    parts[mc] = partial
    part_copies = []
    for d in range(1, nchan):
        copy = pltpu.make_async_remote_copy(
            src_ref=parts.at[mc],
            dst_ref=parts.at[mc],
            send_sem=sp.at[d],
            recv_sem=rp.at[d],
            device_id={"chan": lax.rem(mc + d, nchan)},
            device_id_type=MESH,
        )
        copy.start()
        part_copies.append(copy)

    spill(cnt_out, count)
    for f in range(fields):
        spill(mean_out.at[f], means[f])
        spill(var_out.at[f], variances[f])

    for copy in back_copies:
        copy.wait_recv()
    returned = jnp.concatenate([back_r[d] for d in range(nrows)], axis=0)
    diff_out[...] = unplace(me, nrows, fields, returned, rank_hot, dest)
    for copy in part_copies:
        copy.wait_recv()
    spread = parts[0]
    for c in range(1, nchan):
        spread = spread + parts[c]
    spill(spr_out, spread)
    for copy in scale_copies:
        copy.wait_recv()
    spreads = None
    for e in range(nchan):
        rows = jnp.concatenate([scale_r[e * nrows + d] for d in range(nrows)], axis=0)
        spreads = rows if spreads is None else spreads + rows
    scale_out[...] = lax.rsqrt(1.0 + spreads / CHAN)

    for copy in out_copies + part_copies + back_copies + scale_copies:
        copy.wait_send()


def finish(
    nrows,
    cnt_ref,
    mean_ref,
    var_ref,
    spr_ref,
    diff_ref,
    scale_ref,
    rank_hot,
    band_ref,
    cnt_out,
    mean_out,
    var_out,
    spr_out,
    dep_out,
    sems,
):
    pairs = ((mean_ref, mean_out), (var_ref, var_out), (cnt_ref, cnt_out), (spr_ref, spr_out))
    copies = [pltpu.make_async_copy(a, b, sems.at[i]) for i, (a, b) in enumerate(pairs)]
    for copy in copies:
        copy.start()
    me = lax.axis_index("rows")
    both = dot(jnp.concatenate(two(scale_ref[...]), axis=0).astype(BF16), rank_hot[...], NN)
    merged = both[:nrows] + both[nrows:]
    owner = lax.rem(me + iota((nrows, 1), 0), nrows)
    mine = jnp.where(band_ref[...] == owner, merged, 0.0)
    dep_out[...] = diff_ref[...] * jnp.sum(mine, axis=0, keepdims=True)
    for copy in copies:
        copy.wait()


def body(radiances, band, row_in_band, column):
    nrows = lax.axis_size("rows")
    nchan = lax.axis_size("chan")
    fields, obs = radiances.shape
    cap = 2 * obs // nrows
    nfeat = 1 + 4 * fields
    vmem = pl.BlockSpec(memory_space=pltpu.VMEM)
    anywhere = pl.BlockSpec(memory_space=pl.ANY)
    dma = pltpu.SemaphoreType.DMA
    band = band.reshape(1, obs)
    shapes = (
        ((ROWS_DEV, COLS), jnp.int32),
        ((fields, ROWS_DEV, COLS), F32),
        ((fields, ROWS_DEV, COLS), F32),
        ((ROWS_DEV, COLS), F32),
    )
    held = pl.pallas_call(
        functools.partial(kernel, nrows, nchan),
        out_shape=tuple(pltpu.VMEM(s, t) for s, t in shapes)
        + (
            pltpu.VMEM((fields, obs), F32),
            pltpu.VMEM((nrows, cap), F32),
            pltpu.VMEM((cap, obs), BF16),
            pltpu.VMEM((1, obs), jnp.int32),
        ),
        in_specs=[pl.BlockSpec(memory_space=pltpu.HBM)] * 4,
        out_specs=(vmem,) * 8,
        scratch_shapes=[
            pltpu.VMEM((fields, obs), F32),
            pltpu.VMEM((1, obs), jnp.int32),
            pltpu.VMEM((1, obs), jnp.int32),
            pltpu.VMEM((1, obs), jnp.int32),
            pltpu.VMEM((nrows, LOW, cap), BF16),
            pltpu.VMEM((nrows, QS, cap), F32),
            pltpu.VMEM((nfeat * QS, LOW), F32),
            pltpu.VMEM((nrows, fields, cap), F32),
            pltpu.VMEM((nrows, 1, cap), F32),
            pltpu.VMEM((nrows, fields, cap), F32),
            pltpu.VMEM((nrows, 1, cap), F32),
            pltpu.VMEM((nchan, QS, LOW), F32),
            pltpu.VMEM((nrows, fields, cap), F32),
            pltpu.VMEM((nrows, fields, cap), F32),
            pltpu.VMEM((nrows, 1, cap), F32),
            pltpu.VMEM((nchan * nrows, 1, cap), F32),
            dma((4,)),
            dma((nrows,)),
            dma((nrows,)),
            dma((nrows,)),
            dma((nrows,)),
            dma((nchan,)),
            dma((nchan,)),
            dma((nrows,)),
            dma((nrows,)),
            dma((nchan * nrows,)),
            dma((nchan * nrows,)),
        ],
        compiler_params=pltpu.CompilerParams(
            collective_id=0, has_side_effects=True, vmem_limit_bytes=32 * 1024 * 1024
        ),
    )(
        *(
            pltpu.with_memory_space_constraint(x, pltpu.HBM)
            for x in (radiances, band, row_in_band.reshape(1, obs), column.reshape(1, obs))
        )
    )
    return pl.pallas_call(
        functools.partial(finish, nrows),
        out_shape=tuple(jax.ShapeDtypeStruct(s, t) for s, t in shapes)
        + (jax.ShapeDtypeStruct((fields, obs), F32),),
        in_specs=[vmem] * 8,
        out_specs=(anywhere,) * 4 + (vmem,),
        scratch_shapes=[dma((4,))],
        compiler_params=pltpu.CompilerParams(vmem_limit_bytes=32 * 1024 * 1024),
    )(*held)


def solution(mesh):
    in_specs = (P("chan", "rows"), P("rows", None), P("rows"), P("rows"))
    out_specs = (
        P("rows", None),
        P("chan", "rows", None),
        P("chan", "rows", None),
        P("rows", None),
        P("chan", "rows"),
    )
    return jax.shard_map(body, mesh=mesh, in_specs=in_specs, out_specs=out_specs, check_vma=False)
```

```python
import functools

import jax
import jax.numpy as jnp
from jax import lax
from jax.experimental import pallas as pl
from jax.experimental.pallas import tpu as pltpu
from jax.sharding import PartitionSpec as P

CHAN = 16
COLS = 1440
ROWS_DEV = 4
LOW = 256
LANES = 128
BLOCKS = -(-COLS // LOW)
QS = BLOCKS * ROWS_DEV
F32 = jnp.float32
BF16 = jnp.bfloat16
MESH = pl.DeviceIdType.MESH
NT = (((1,), (1,)), ((), ()))
NN = (((1,), (0,)), ((), ()))


def iota(shape, axis):
    return lax.broadcasted_iota(jnp.int32, shape, axis)


def onehot(mask):
    return jnp.where(mask, 1.0, 0.0)


def two(values):
    high = values.astype(BF16).astype(F32)
    return high, values - high


def dot(a, b, dims):
    return lax.dot_general(a, b, dims, preferred_element_type=F32)


def rank_of(dest, nrows):
    obs = dest.shape[1]
    nblock = obs // 128
    hot = onehot(iota((nrows, obs), 0) == dest)
    stacked = jnp.concatenate([hot[:, b * 128 : (b + 1) * 128] for b in range(nblock)], axis=0)
    stacked_b = stacked.astype(BF16)
    size = nblock * nrows
    upper = onehot(iota((128, 128), 0) <= iota((128, 128), 1)).astype(BF16)
    inner = dot(stacked_b, upper, NN)
    r, c = iota((size, size), 0), iota((size, size), 1)
    earlier = onehot((c < r) & (lax.rem(r - c + size, nrows) == 0)).astype(BF16)
    before = jnp.sum(dot(earlier, stacked_b, NN), axis=1, keepdims=True)
    ranks = stacked * (inner + before)
    rows = [
        jnp.sum(ranks[b * nrows : (b + 1) * nrows], axis=0, keepdims=True) for b in range(nblock)
    ]
    return (jnp.concatenate(rows, axis=1) - 1.0).astype(jnp.int32)


def spill(out, values):
    for j in range(BLOCKS):
        start = j * LOW
        width = min(LOW, COLS - start)
        out[:, start : start + width] = values[j * ROWS_DEV : (j + 1) * ROWS_DEV, :width].astype(
            out.dtype
        )


def kernel(
    nrows,
    nchan,
    rad_in,
    band_in,
    rib_in,
    col_in,
    cnt_out,
    mean_out,
    var_out,
    spr_out,
    diff_out,
    scale_out,
    rank_out,
    dest_out,
    rank_hot,
    rad_ref,
    band_ref,
    rib_ref,
    col_ref,
    col_hot,
    q_hot,
    acc,
    send_v,
    send_c,
    recv_v,
    recv_c,
    parts,
    back_s,
    back_r,
    scale_s,
    scale_r,
    ins,
    sv,
    rv,
    sc,
    rc,
    sp,
    rp,
    sb,
    rb,
    ss,
    rs,
):
    me = lax.axis_index("rows")
    mc = lax.axis_index("chan")
    fields, obs = rad_ref.shape
    cap = rank_hot.shape[0]

    fetches = [
        pltpu.make_async_copy(a, b, ins.at[i])
        for i, (a, b) in enumerate(
            ((band_in, band_ref), (rad_in, rad_ref), (rib_in, rib_ref), (col_in, col_ref))
        )
    ]
    for fetch in fetches:
        fetch.start()
    barrier = pltpu.get_barrier_semaphore()
    for d in range(nrows):
        for e in range(nchan):
            if d + e > 0:
                to = {"rows": lax.rem(me + d, nrows), "chan": lax.rem(mc + e, nchan)}
                pl.semaphore_signal(barrier, inc=1, device_id=to, device_id_type=MESH)

    fetches[0].wait()
    dest = band_ref[...]
    dest_out[...] = dest
    rank = rank_of(dest, nrows)
    rank_out[...] = rank
    rank_hot[...] = onehot(iota((cap, obs), 0) == rank).astype(BF16)
    for fetch in fetches[1:]:
        fetch.wait()
    rad = rad_ref[...]
    high, rest = two(rad)
    middle, low = two(rest)
    col = col_ref[...]
    code = (col // LOW) * ROWS_DEV + rib_ref[...] + 1
    pad = -(3 * fields + 2) % 8
    group = 3 * fields + 2 + pad
    payload = jnp.concatenate(
        [high, middle, low, code.astype(F32), (col % LOW).astype(F32), jnp.zeros((pad, obs), F32)],
        axis=0,
    )
    left = jnp.concatenate(
        [jnp.where(dest == lax.rem(me + d, nrows), payload, 0.0) for d in range(nrows)], axis=0
    ).astype(BF16)
    placed = dot(left, rank_hot[...], NT)
    pl.semaphore_wait(barrier, nrows * nchan - 1)

    out_copies = []
    for d in list(range(1, nrows)) + [0]:
        part = placed[d * group : (d + 1) * group]
        values = (part[:fields] + part[fields : 2 * fields]) + part[2 * fields : 3 * fields]
        cells = part[3 * fields : 3 * fields + 1] * LOW + part[3 * fields + 1 : 3 * fields + 2]
        if d == 0:
            recv_v[0] = values
            recv_c[0] = cells
            continue
        send_v[d] = values
        send_c[d] = cells
        to = {"rows": lax.rem(me + d, nrows)}
        for src, dst, s, r in ((send_v, recv_v, sv, rv), (send_c, recv_c, sc, rc)):
            copy = pltpu.make_async_remote_copy(
                src_ref=src.at[d],
                dst_ref=dst.at[d],
                send_sem=s.at[d],
                recv_sem=r.at[d],
                device_id=to,
                device_id_type=MESH,
            )
            copy.start()
            out_copies.append(copy)

    for d in range(nrows):
        if d > 0:
            out_copies[2 * d - 2].wait_recv()
            out_copies[2 * d - 1].wait_recv()
        values = recv_v[d]
        cells = recv_c[d].astype(jnp.int32)
        cols_t = onehot(iota((LOW, cap), 0) == (cells & (LOW - 1))).astype(BF16)
        col_hot[d] = cols_t
        quads = onehot(iota((QS, cap), 0) == (cells // LOW) - 1)
        q_hot[d] = quads
        features = two(values) + two(values * values)
        rows = [quads] + [quads * x[f : f + 1] for x in features for f in range(fields)]
        sums = dot(jnp.concatenate(rows, axis=0).astype(BF16), cols_t, NT)
        if d == 0:
            acc[...] = sums
        else:
            acc[...] += sums

    count = acc[0:QS]
    inverse = 1.0 / jnp.maximum(count, 1.0)
    means, variances = [], []
    for f in range(fields):

        def total(k):
            at = (1 + k * fields + f) * QS
            after = at + fields * QS
            return acc[at : at + QS] + acc[after : after + QS]

        mean = total(0) * inverse
        means.append(mean)
        variances.append(jnp.maximum(total(2) * inverse - mean * mean, 0.0))
    partial = variances[0]
    for f in range(1, fields):
        partial = partial + variances[f]
    split = [two(mean) for mean in means]
    table = jnp.concatenate([x[0] for x in split] + [x[1] for x in split], axis=0).astype(BF16)
    back_copies = []
    for d in list(range(1, nrows)) + [0]:
        picked = dot(table, col_hot[d], NN)
        quads = q_hot[d]
        found = []
        for f in range(fields):
            at = (fields + f) * QS
            both = picked[f * QS : (f + 1) * QS] + picked[at : at + QS]
            found.append(jnp.sum(both * quads, axis=0, keepdims=True))
        diff = recv_v[d] - jnp.concatenate(found, axis=0)
        if d == 0:
            back_r[0] = diff
            continue
        back_s[d] = diff
        copy = pltpu.make_async_remote_copy(
            src_ref=back_s.at[d],
            dst_ref=back_r.at[d],
            send_sem=sb.at[d],
            recv_sem=rb.at[d],
            device_id={"rows": lax.rem(me + nrows - d, nrows)},
            device_id_type=MESH,
        )
        copy.start()
        back_copies.append(copy)

    table = jnp.concatenate(two(partial), axis=0).astype(BF16)
    scale_copies = []
    for d in list(range(1, nrows)) + [0]:
        picked = dot(table, col_hot[d], NN)
        found = jnp.sum((picked[:QS] + picked[QS:]) * q_hot[d], axis=0, keepdims=True)
        scale_s[d] = found
        if d == 0:
            scale_r[0] = found
        for e in range(nchan):
            if d + e == 0:
                continue
            slot = e * nrows + d
            copy = pltpu.make_async_remote_copy(
                src_ref=scale_s.at[d],
                dst_ref=scale_r.at[slot],
                send_sem=ss.at[slot],
                recv_sem=rs.at[slot],
                device_id={
                    "rows": lax.rem(me + nrows - d, nrows),
                    "chan": lax.rem(mc + e, nchan),
                },
                device_id_type=MESH,
            )
            copy.start()
            scale_copies.append(copy)
    parts[mc] = partial
    part_copies = []
    for d in range(1, nchan):
        copy = pltpu.make_async_remote_copy(
            src_ref=parts.at[mc],
            dst_ref=parts.at[mc],
            send_sem=sp.at[d],
            recv_sem=rp.at[d],
            device_id={"chan": lax.rem(mc + d, nchan)},
            device_id_type=MESH,
        )
        copy.start()
        part_copies.append(copy)

    spill(cnt_out, count)
    for f in range(fields):
        spill(mean_out.at[f], means[f])
        spill(var_out.at[f], variances[f])

    for copy in back_copies:
        copy.wait_recv()
    diff_out[...] = back_r[...]
    for copy in part_copies:
        copy.wait_recv()
    spread = parts[0]
    for c in range(1, nchan):
        spread = spread + parts[c]
    spill(spr_out, spread)
    for copy in scale_copies:
        copy.wait_recv()
    spreads = None
    for e in range(nchan):
        rows = jnp.concatenate([scale_r[e * nrows + d] for d in range(nrows)], axis=0)
        spreads = rows if spreads is None else spreads + rows
    scale_out[...] = lax.rsqrt(1.0 + spreads / CHAN)

    for copy in out_copies + part_copies + back_copies + scale_copies:
        copy.wait_send()


def finish(
    nrows,
    cnt_ref,
    mean_ref,
    var_ref,
    spr_ref,
    diff_ref,
    scale_ref,
    rank_ref,
    dest_ref,
    cnt_out,
    mean_out,
    var_out,
    spr_out,
    dep_out,
    sems,
):
    pairs = ((mean_ref, mean_out), (var_ref, var_out), (cnt_ref, cnt_out), (spr_ref, spr_out))
    copies = [pltpu.make_async_copy(a, b, sems.at[i]) for i, (a, b) in enumerate(pairs)]
    for copy in copies:
        copy.start()
    me = lax.axis_index("rows")
    fields, obs = dep_out.shape
    tiles = -(-scale_ref.shape[1] // LANES)
    lines = obs // LANES

    def folded(ref):
        return jnp.concatenate(
            [ref[:, k * LANES : (k + 1) * LANES] for k in range(lines)], axis=0
        )

    rank = folded(rank_ref)
    distance = lax.rem(folded(dest_ref) - me + nrows, nrows)
    place = distance * tiles + rank // LANES
    lane = rank & (LANES - 1)
    found = [jnp.zeros((lines, LANES), F32) for _ in range(fields + 1)]
    for d in range(nrows):
        for t in range(tiles):
            here = place == d * tiles + t
            span = slice(t * LANES, (t + 1) * LANES)
            for f in range(fields + 1):
                row = scale_ref[d : d + 1, span] if f == fields else diff_ref[d, f : f + 1, span]
                taken = jnp.take_along_axis(
                    jnp.broadcast_to(row, (lines, LANES)), lane, axis=1, mode="promise_in_bounds"
                )
                found[f] = jnp.where(here, taken, found[f])
    results = [found[f] * found[fields] for f in range(fields)]
    for k in range(lines):
        dep_out[:, k * LANES : (k + 1) * LANES] = jnp.concatenate(
            [x[k : k + 1] for x in results], axis=0
        )
    for copy in copies:
        copy.wait()


def body(radiances, band, row_in_band, column):
    nrows = lax.axis_size("rows")
    nchan = lax.axis_size("chan")
    fields, obs = radiances.shape
    cap = 2 * obs // nrows
    nfeat = 1 + 4 * fields
    vmem = pl.BlockSpec(memory_space=pltpu.VMEM)
    anywhere = pl.BlockSpec(memory_space=pl.ANY)
    dma = pltpu.SemaphoreType.DMA
    band = band.reshape(1, obs)
    shapes = (
        ((ROWS_DEV, COLS), jnp.int32),
        ((fields, ROWS_DEV, COLS), F32),
        ((fields, ROWS_DEV, COLS), F32),
        ((ROWS_DEV, COLS), F32),
    )
    held = pl.pallas_call(
        functools.partial(kernel, nrows, nchan),
        out_shape=tuple(pltpu.VMEM(s, t) for s, t in shapes)
        + (
            pltpu.VMEM((nrows, fields, cap), F32),
            pltpu.VMEM((nrows, cap), F32),
            pltpu.VMEM((1, obs), jnp.int32),
            pltpu.VMEM((1, obs), jnp.int32),
        ),
        in_specs=[pl.BlockSpec(memory_space=pltpu.HBM)] * 4,
        out_specs=(vmem,) * 8,
        scratch_shapes=[
            pltpu.VMEM((cap, obs), BF16),
            pltpu.VMEM((fields, obs), F32),
            pltpu.VMEM((1, obs), jnp.int32),
            pltpu.VMEM((1, obs), jnp.int32),
            pltpu.VMEM((1, obs), jnp.int32),
            pltpu.VMEM((nrows, LOW, cap), BF16),
            pltpu.VMEM((nrows, QS, cap), F32),
            pltpu.VMEM((nfeat * QS, LOW), F32),
            pltpu.VMEM((nrows, fields, cap), F32),
            pltpu.VMEM((nrows, 1, cap), F32),
            pltpu.VMEM((nrows, fields, cap), F32),
            pltpu.VMEM((nrows, 1, cap), F32),
            pltpu.VMEM((nchan, QS, LOW), F32),
            pltpu.VMEM((nrows, fields, cap), F32),
            pltpu.VMEM((nrows, fields, cap), F32),
            pltpu.VMEM((nrows, 1, cap), F32),
            pltpu.VMEM((nchan * nrows, 1, cap), F32),
            dma((4,)),
            dma((nrows,)),
            dma((nrows,)),
            dma((nrows,)),
            dma((nrows,)),
            dma((nchan,)),
            dma((nchan,)),
            dma((nrows,)),
            dma((nrows,)),
            dma((nchan * nrows,)),
            dma((nchan * nrows,)),
        ],
        compiler_params=pltpu.CompilerParams(
            collective_id=0, has_side_effects=True, vmem_limit_bytes=32 * 1024 * 1024
        ),
    )(
        *(
            pltpu.with_memory_space_constraint(x, pltpu.HBM)
            for x in (radiances, band, row_in_band.reshape(1, obs), column.reshape(1, obs))
        )
    )
    return pl.pallas_call(
        functools.partial(finish, nrows),
        out_shape=tuple(jax.ShapeDtypeStruct(s, t) for s, t in shapes)
        + (jax.ShapeDtypeStruct((fields, obs), F32),),
        in_specs=[vmem] * 8,
        out_specs=(anywhere,) * 4 + (vmem,),
        scratch_shapes=[dma((4,))],
        compiler_params=pltpu.CompilerParams(vmem_limit_bytes=32 * 1024 * 1024),
    )(*held)


def solution(mesh):
    in_specs = (P("chan", "rows"), P("rows", None), P("rows"), P("rows"))
    out_specs = (
        P("rows", None),
        P("chan", "rows", None),
        P("chan", "rows", None),
        P("rows", None),
        P("chan", "rows"),
    )
    return jax.shard_map(body, mesh=mesh, in_specs=in_specs, out_specs=out_specs, check_vma=False)
```

```python
import functools

import jax
import jax.numpy as jnp
from jax import lax
from jax.experimental import pallas as pl
from jax.experimental.pallas import tpu as pltpu
from jax.sharding import PartitionSpec as P

CHAN = 16
COLS = 1440
ROWS_DEV = 4
LOW = 256
LANES = 128
BLOCKS = -(-COLS // LOW)
QS = BLOCKS * ROWS_DEV
F32 = jnp.float32
BF16 = jnp.bfloat16
MESH = pl.DeviceIdType.MESH
NT = (((1,), (1,)), ((), ()))
NN = (((1,), (0,)), ((), ()))


def iota(shape, axis):
    return lax.broadcasted_iota(jnp.int32, shape, axis)


def onehot(mask):
    return jnp.where(mask, 1.0, 0.0)


def two(values):
    high = values.astype(BF16).astype(F32)
    return high, values - high


def dot(a, b, dims):
    return lax.dot_general(a, b, dims, preferred_element_type=F32)


def rank_of(dest, nrows):
    obs = dest.shape[1]
    nblock = obs // 128
    hot = onehot(iota((nrows, obs), 0) == dest)
    stacked = jnp.concatenate([hot[:, b * 128 : (b + 1) * 128] for b in range(nblock)], axis=0)
    stacked_b = stacked.astype(BF16)
    size = nblock * nrows
    upper = onehot(iota((128, 128), 0) <= iota((128, 128), 1)).astype(BF16)
    inner = dot(stacked_b, upper, NN)
    r, c = iota((size, size), 0), iota((size, size), 1)
    earlier = onehot((c < r) & (lax.rem(r - c + size, nrows) == 0)).astype(BF16)
    before = jnp.sum(dot(earlier, stacked_b, NN), axis=1, keepdims=True)
    ranks = stacked * (inner + before)
    rows = [
        jnp.sum(ranks[b * nrows : (b + 1) * nrows], axis=0, keepdims=True) for b in range(nblock)
    ]
    return (jnp.concatenate(rows, axis=1) - 1.0).astype(jnp.int32)


def spill(out, values):
    for j in range(BLOCKS):
        start = j * LOW
        width = min(LOW, COLS - start)
        out[:, start : start + width] = values[j * ROWS_DEV : (j + 1) * ROWS_DEV, :width].astype(
            out.dtype
        )


def kernel(
    nrows,
    nchan,
    rad_in,
    band_in,
    rib_in,
    col_in,
    cnt_out,
    mean_out,
    var_out,
    spr_out,
    diff_out,
    scale_out,
    rank_out,
    dest_out,
    rank_hot,
    rad_ref,
    band_ref,
    rib_ref,
    col_ref,
    col_hot,
    q_hot,
    acc,
    send_v,
    send_c,
    recv_v,
    recv_c,
    parts,
    back_s,
    back_r,
    scale_s,
    scale_r,
    ins,
    sv,
    rv,
    sc,
    rc,
    sp,
    rp,
    sb,
    rb,
    ss,
    rs,
):
    me = lax.axis_index("rows")
    mc = lax.axis_index("chan")
    fields, obs = rad_ref.shape
    cap = rank_hot.shape[0]

    fetches = [
        pltpu.make_async_copy(a, b, ins.at[i])
        for i, (a, b) in enumerate(
            ((band_in, band_ref), (rad_in, rad_ref), (rib_in, rib_ref), (col_in, col_ref))
        )
    ]
    for fetch in fetches:
        fetch.start()
    barrier = pltpu.get_barrier_semaphore()
    for d in range(nrows):
        for e in range(nchan):
            if d + e > 0:
                to = {"rows": lax.rem(me + d, nrows), "chan": lax.rem(mc + e, nchan)}
                pl.semaphore_signal(barrier, inc=1, device_id=to, device_id_type=MESH)

    fetches[0].wait()
    dest = band_ref[...]
    dest_out[...] = dest
    rank = rank_of(dest, nrows)
    rank_out[...] = rank
    rank_hot[...] = onehot(iota((cap, obs), 0) == rank).astype(BF16)
    for fetch in fetches[1:]:
        fetch.wait()
    rad = rad_ref[...]
    high, rest = two(rad)
    middle, low = two(rest)
    col = col_ref[...]
    code = (col // LOW) * ROWS_DEV + rib_ref[...] + 1
    pad = -(3 * fields + 2) % 8
    group = 3 * fields + 2 + pad
    payload = jnp.concatenate(
        [high, middle, low, code.astype(F32), (col % LOW).astype(F32), jnp.zeros((pad, obs), F32)],
        axis=0,
    )
    left = jnp.concatenate(
        [jnp.where(dest == lax.rem(me + d, nrows), payload, 0.0) for d in range(nrows)], axis=0
    ).astype(BF16)
    placed = dot(left, rank_hot[...], NT)
    pl.semaphore_wait(barrier, nrows * nchan - 1)

    out_copies = []
    for d in list(range(1, nrows)) + [0]:
        part = placed[d * group : (d + 1) * group]
        values = (part[:fields] + part[fields : 2 * fields]) + part[2 * fields : 3 * fields]
        cells = part[3 * fields : 3 * fields + 1] * LOW + part[3 * fields + 1 : 3 * fields + 2]
        if d == 0:
            recv_v[0] = values
            recv_c[0] = cells
            continue
        send_v[d] = values
        send_c[d] = cells
        to = {"rows": lax.rem(me + d, nrows)}
        for src, dst, s, r in ((send_v, recv_v, sv, rv), (send_c, recv_c, sc, rc)):
            copy = pltpu.make_async_remote_copy(
                src_ref=src.at[d],
                dst_ref=dst.at[d],
                send_sem=s.at[d],
                recv_sem=r.at[d],
                device_id=to,
                device_id_type=MESH,
            )
            copy.start()
            out_copies.append(copy)

    for d in range(nrows):
        if d > 0:
            out_copies[2 * d - 2].wait_recv()
            out_copies[2 * d - 1].wait_recv()
        values = recv_v[d]
        cells = recv_c[d].astype(jnp.int32)
        cols_t = onehot(iota((LOW, cap), 0) == (cells & (LOW - 1))).astype(BF16)
        col_hot[d] = cols_t
        quads = onehot(iota((QS, cap), 0) == (cells // LOW) - 1)
        q_hot[d] = quads
        features = two(values) + two(values * values)
        rows = [quads] + [quads * x[f : f + 1] for x in features for f in range(fields)]
        sums = dot(jnp.concatenate(rows, axis=0).astype(BF16), cols_t, NT)
        if d == 0:
            acc[...] = sums
        else:
            acc[...] += sums

    count = acc[0:QS]
    inverse = 1.0 / jnp.maximum(count, 1.0)
    means, variances = [], []
    for f in range(fields):

        def total(k):
            at = (1 + k * fields + f) * QS
            after = at + fields * QS
            return acc[at : at + QS] + acc[after : after + QS]

        mean = total(0) * inverse
        means.append(mean)
        variances.append(jnp.maximum(total(2) * inverse - mean * mean, 0.0))
    partial = variances[0]
    for f in range(1, fields):
        partial = partial + variances[f]
    split = [two(mean) for mean in means]
    split.append(two(partial))
    table = jnp.concatenate([x[0] for x in split] + [x[1] for x in split], axis=0).astype(BF16)
    back_copies = []
    scale_copies = []
    for d in list(range(1, nrows)) + [0]:
        picked = dot(table, col_hot[d], NN)
        quads = q_hot[d]
        found = []
        for f in range(fields + 1):
            at = (fields + 1 + f) * QS
            both = picked[f * QS : (f + 1) * QS] + picked[at : at + QS]
            found.append(jnp.sum(both * quads, axis=0, keepdims=True))
        diff = recv_v[d] - jnp.concatenate(found[:fields], axis=0)
        scale_s[d] = found[fields]
        if d == 0:
            back_r[0] = diff
            scale_r[0] = found[fields]
        if d > 0:
            back_s[d] = diff
            copy = pltpu.make_async_remote_copy(
                src_ref=back_s.at[d],
                dst_ref=back_r.at[d],
                send_sem=sb.at[d],
                recv_sem=rb.at[d],
                device_id={"rows": lax.rem(me + nrows - d, nrows)},
                device_id_type=MESH,
            )
            copy.start()
            back_copies.append(copy)
        for e in range(nchan):
            if d + e == 0:
                continue
            slot = e * nrows + d
            copy = pltpu.make_async_remote_copy(
                src_ref=scale_s.at[d],
                dst_ref=scale_r.at[slot],
                send_sem=ss.at[slot],
                recv_sem=rs.at[slot],
                device_id={
                    "rows": lax.rem(me + nrows - d, nrows),
                    "chan": lax.rem(mc + e, nchan),
                },
                device_id_type=MESH,
            )
            copy.start()
            scale_copies.append(copy)

    parts[mc] = partial
    part_copies = []
    for d in range(1, nchan):
        copy = pltpu.make_async_remote_copy(
            src_ref=parts.at[mc],
            dst_ref=parts.at[mc],
            send_sem=sp.at[d],
            recv_sem=rp.at[d],
            device_id={"chan": lax.rem(mc + d, nchan)},
            device_id_type=MESH,
        )
        copy.start()
        part_copies.append(copy)

    spill(cnt_out, count)
    for f in range(fields):
        spill(mean_out.at[f], means[f])
        spill(var_out.at[f], variances[f])

    for copy in back_copies:
        copy.wait_recv()
    diff_out[...] = back_r[...]
    for copy in part_copies:
        copy.wait_recv()
    spread = parts[0]
    for c in range(1, nchan):
        spread = spread + parts[c]
    spill(spr_out, spread)
    for copy in scale_copies:
        copy.wait_recv()
    spreads = None
    for e in range(nchan):
        rows = jnp.concatenate([scale_r[e * nrows + d] for d in range(nrows)], axis=0)
        spreads = rows if spreads is None else spreads + rows
    scale_out[...] = lax.rsqrt(1.0 + spreads / CHAN)

    for copy in out_copies + part_copies + back_copies + scale_copies:
        copy.wait_send()


def finish(
    nrows,
    cnt_ref,
    mean_ref,
    var_ref,
    spr_ref,
    diff_ref,
    scale_ref,
    rank_ref,
    dest_ref,
    cnt_out,
    mean_out,
    var_out,
    spr_out,
    dep_out,
    sems,
):
    pairs = ((mean_ref, mean_out), (var_ref, var_out), (cnt_ref, cnt_out), (spr_ref, spr_out))
    copies = [pltpu.make_async_copy(a, b, sems.at[i]) for i, (a, b) in enumerate(pairs)]
    for copy in copies:
        copy.start()
    me = lax.axis_index("rows")
    fields, obs = dep_out.shape
    tiles = -(-scale_ref.shape[1] // LANES)
    lines = obs // LANES

    def folded(ref):
        return jnp.concatenate(
            [ref[:, k * LANES : (k + 1) * LANES] for k in range(lines)], axis=0
        )

    rank = folded(rank_ref)
    distance = lax.rem(folded(dest_ref) - me + nrows, nrows)
    place = distance * tiles + rank // LANES
    lane = rank & (LANES - 1)
    found = [jnp.zeros((lines, LANES), F32) for _ in range(fields + 1)]
    for d in range(nrows):
        for t in range(tiles):
            here = place == d * tiles + t
            span = slice(t * LANES, (t + 1) * LANES)
            for f in range(fields + 1):
                row = scale_ref[d : d + 1, span] if f == fields else diff_ref[d, f : f + 1, span]
                taken = jnp.take_along_axis(
                    jnp.broadcast_to(row, (lines, LANES)), lane, axis=1, mode="promise_in_bounds"
                )
                found[f] = jnp.where(here, taken, found[f])
    results = [found[f] * found[fields] for f in range(fields)]
    for k in range(lines):
        dep_out[:, k * LANES : (k + 1) * LANES] = jnp.concatenate(
            [x[k : k + 1] for x in results], axis=0
        )
    for copy in copies:
        copy.wait()


def body(radiances, band, row_in_band, column):
    nrows = lax.axis_size("rows")
    nchan = lax.axis_size("chan")
    fields, obs = radiances.shape
    cap = 2 * obs // nrows
    nfeat = 1 + 4 * fields
    vmem = pl.BlockSpec(memory_space=pltpu.VMEM)
    anywhere = pl.BlockSpec(memory_space=pl.ANY)
    dma = pltpu.SemaphoreType.DMA
    band = band.reshape(1, obs)
    shapes = (
        ((ROWS_DEV, COLS), jnp.int32),
        ((fields, ROWS_DEV, COLS), F32),
        ((fields, ROWS_DEV, COLS), F32),
        ((ROWS_DEV, COLS), F32),
    )
    held = pl.pallas_call(
        functools.partial(kernel, nrows, nchan),
        out_shape=tuple(pltpu.VMEM(s, t) for s, t in shapes)
        + (
            pltpu.VMEM((nrows, fields, cap), F32),
            pltpu.VMEM((nrows, cap), F32),
            pltpu.VMEM((1, obs), jnp.int32),
            pltpu.VMEM((1, obs), jnp.int32),
        ),
        in_specs=[pl.BlockSpec(memory_space=pltpu.HBM)] * 4,
        out_specs=(vmem,) * 8,
        scratch_shapes=[
            pltpu.VMEM((cap, obs), BF16),
            pltpu.VMEM((fields, obs), F32),
            pltpu.VMEM((1, obs), jnp.int32),
            pltpu.VMEM((1, obs), jnp.int32),
            pltpu.VMEM((1, obs), jnp.int32),
            pltpu.VMEM((nrows, LOW, cap), BF16),
            pltpu.VMEM((nrows, QS, cap), F32),
            pltpu.VMEM((nfeat * QS, LOW), F32),
            pltpu.VMEM((nrows, fields, cap), F32),
            pltpu.VMEM((nrows, 1, cap), F32),
            pltpu.VMEM((nrows, fields, cap), F32),
            pltpu.VMEM((nrows, 1, cap), F32),
            pltpu.VMEM((nchan, QS, LOW), F32),
            pltpu.VMEM((nrows, fields, cap), F32),
            pltpu.VMEM((nrows, fields, cap), F32),
            pltpu.VMEM((nrows, 1, cap), F32),
            pltpu.VMEM((nchan * nrows, 1, cap), F32),
            dma((4,)),
            dma((nrows,)),
            dma((nrows,)),
            dma((nrows,)),
            dma((nrows,)),
            dma((nchan,)),
            dma((nchan,)),
            dma((nrows,)),
            dma((nrows,)),
            dma((nchan * nrows,)),
            dma((nchan * nrows,)),
        ],
        compiler_params=pltpu.CompilerParams(
            collective_id=0, has_side_effects=True, vmem_limit_bytes=32 * 1024 * 1024
        ),
    )(
        *(
            pltpu.with_memory_space_constraint(x, pltpu.HBM)
            for x in (radiances, band, row_in_band.reshape(1, obs), column.reshape(1, obs))
        )
    )
    return pl.pallas_call(
        functools.partial(finish, nrows),
        out_shape=tuple(jax.ShapeDtypeStruct(s, t) for s, t in shapes)
        + (jax.ShapeDtypeStruct((fields, obs), F32),),
        in_specs=[vmem] * 8,
        out_specs=(anywhere,) * 4 + (vmem,),
        scratch_shapes=[dma((4,))],
        compiler_params=pltpu.CompilerParams(vmem_limit_bytes=32 * 1024 * 1024),
    )(*held)


def solution(mesh):
    in_specs = (P("chan", "rows"), P("rows", None), P("rows"), P("rows"))
    out_specs = (
        P("rows", None),
        P("chan", "rows", None),
        P("chan", "rows", None),
        P("rows", None),
        P("chan", "rows"),
    )
    return jax.shard_map(body, mesh=mesh, in_specs=in_specs, out_specs=out_specs, check_vma=False)
```
